1024 devices in a mesh: pitch: 64 (over z_hi, y, core), span: 16 (over z_lo, x).
Axes of the slice: x: 4, y: 8, z: 16 (z_hi: 4, z_lo: 4; z = z_hi * 4 + z_lo), core: 2. Of those that a mesh axis runs over, the one named last changes fastest.
Arguments:
- state: float32 [5, 5, 5, 5, 128, 16, 128], P(None, None, None, None, 'pitch', 'span'), may hold values from -6 to 6
- wake_planes: float32 [5, 5, 5, 128, 16], P(None, None, None, 'pitch', 'span'), may hold values from -6 to 6
- bar_offsets: int32 [3], replicated, may hold values from 0 to 1, as said below
Outputs:
- advanced: float32 [5, 5, 5, 5, 128, 16, 128], P(None, None, None, None, 'pitch', 'span')
The draws below stay inside these ranges and needn't reach their ends.
Inputs may be any that keep to these rules, and one draw needn't show every extreme that they name: `bar_offsets`: some section has offset 1 and some section offset 0.
All inputs are finite; a program needn't handle non-finite values.
Results may differ from the reference program's by a relative error of at most 0.0001.
Values sent between devices are 32-bit elements; how exact they have to be, the bound alone decides.
A program may use at most 64 MiB of HBM per device.

```python
import jax
import jax.numpy as jnp
import numpy as np
from jax import lax

VARS = 5
NODES = 5
SECTIONS = 3
EP = 2
EA = 128
EPT = 128
EST = 16


def draw_bar_offsets(key, part):
    first_key, second_key = jax.random.split(key)
    values = jax.random.randint(first_key, (SECTIONS,), 0, EP)
    which = jax.random.randint(second_key, (), 0, SECTIONS)
    values = values.at[which].set(EP - 1)
    values = values.at[(which + 1) % SECTIONS].set(0)
    return values.astype(jnp.int32)


def level_of(key, dims, shards, least, top_value):
    factor_of = 1.0
    for dim, shards_of in shards:
        heights = jax.random.uniform(jax.random.fold_in(jax.random.fold_in(key, 6), dim), (shards_of,), jnp.float32, least / len(shards), top_value / len(shards))
        factor_of = factor_of * jnp.repeat(jnp.exp(heights), dims[dim] // shards_of).reshape((-1,) + (1,) * (len(dims) - 1 - dim))
    return factor_of


def gaussian(own_key, shape, width, limit, shards=(), kind=jnp.bfloat16):
    entries = jax.random.normal(own_key, shape, jnp.float32) * width
    if len(shards) > 0:
        entries = level_of(own_key, shape, shards, -0.22, 0.18) * entries
    return jnp.clip(entries, min=-limit, max=limit).astype(kind)


def setup_inputs(seed: int = 0) -> dict:
    seeds = jax.random.split(jax.random.key(seed), 4)
    state = gaussian(seeds[0], (VARS, NODES, NODES, NODES, EPT, EST, EA), 1.0, 6.0, ((4, 64), (5, 16)), jnp.float32)
    wake_planes = gaussian(seeds[1], (VARS, NODES, NODES, EPT, EST), 1.0, 6.0, ((3, 64), (4, 16)), jnp.float32)
    bar_offsets = draw_bar_offsets(jax.random.fold_in(seeds[3], 71), 0)
    return dict(state=state, wake_planes=wake_planes, bar_offsets=bar_offsets)


MEAN_FLOW = (0.5, 0.3, 0.0)
WAVE_SPEED = (1.5, 1.3, 1.0)
ELEM_SIZE = (1.0, 0.8, 1.2)
END_WEIGHT = 0.1
TIME_STEP = 0.01
FORMS = ('ij,vjbcxyz->vibcxyz', 'ij,vajcxyz->vaicxyz', 'ij,vabjxyz->vabixyz')

def derivative_matrix():
    points = np.array([-1.0, -np.sqrt(3.0 / 7.0), 0.0, np.sqrt(3.0 / 7.0), 1.0])
    products = np.array([np.prod([points[j] - points[k] for k in range(5) if k != j]) for j in range(5)])
    matrix = np.zeros((5, 5))
    for i in range(5):
        for j in range(5):
            if i != j:
                matrix[i, j] = products[i] / (products[j] * (points[i] - points[j]))
        matrix[i, i] = sum((1.0 / (points[i] - points[k]) for k in range(5) if k != i))
    return jnp.asarray(matrix, dtype=jnp.float32)

def physical_flux(values, direction):
    mean_speed = MEAN_FLOW[direction]
    pieces = [mean_speed * values[v] for v in range(5)]
    normal_vel = values[1 + direction]
    pieces[0] = pieces[0] + normal_vel
    pieces[4] = pieces[4] + normal_vel
    pieces[1 + direction] = pieces[1 + direction] + values[4]
    return jnp.stack(pieces)

def interface_flux(left_state, right_state, direction):
    both_sides = physical_flux(left_state, direction) + physical_flux(right_state, direction)
    return 0.5 * both_sides - 0.5 * WAVE_SPEED[direction] * (right_state - left_state)

def volume_term(state, matrix):
    tendency = None
    for direction in range(3):
        derived = jnp.einsum(FORMS[direction], matrix, physical_flux(state, direction), precision=lax.Precision.HIGHEST)
        term = -(2.0 / ELEM_SIZE[direction]) * derived
        tendency = term if direction == 0 else tendency + term
    return tendency

def face_traces(state, direction):
    upper_trace = lax.index_in_dim(state, 4, 1 + direction, keepdims=False)
    lower_trace = lax.index_in_dim(state, 0, 1 + direction, keepdims=False)
    return (upper_trace, lower_trace)

def add_faces(tendency, upper_trace, lower_trace, upper_flux, lower_flux, direction):
    factor = 2.0 / (ELEM_SIZE[direction] * END_WEIGHT)
    lift_upper = factor * (physical_flux(upper_trace, direction) - upper_flux)
    lift_lower = factor * (lower_flux - physical_flux(lower_trace, direction))
    leading = (slice(None),) * (1 + direction)
    tendency = tendency.at[leading + (4,)].add(lift_upper)
    return tendency.at[leading + (0,)].add(lift_lower)

def tendency_of(state, matrix, inlet):
    tendency = volume_term(state, matrix)
    upper_trace, lower_trace = face_traces(state, 0)
    count = upper_trace.shape[5]
    next_trace = jnp.concatenate([lax.slice_in_dim(lower_trace, 1, count, axis=5), lax.slice_in_dim(upper_trace, count - 1, count, axis=5)], axis=5)
    prev_trace = jnp.concatenate([inlet[..., None], lax.slice_in_dim(upper_trace, 0, count - 1, axis=5)], axis=5)
    tendency = add_faces(tendency, upper_trace, lower_trace, interface_flux(upper_trace, next_trace, 0), interface_flux(prev_trace, lower_trace, 0), 0)
    upper_trace, lower_trace = face_traces(state, 1)
    next_trace = jnp.roll(lower_trace, -1, axis=3)
    prev_trace = jnp.roll(upper_trace, 1, axis=3)
    tendency = add_faces(tendency, upper_trace, lower_trace, interface_flux(upper_trace, next_trace, 1), interface_flux(prev_trace, lower_trace, 1), 1)
    upper_trace, lower_trace = face_traces(state, 2)
    count = upper_trace.shape[4]
    empty = jnp.zeros_like(lax.slice_in_dim(lower_trace, 0, 1, axis=4))
    next_trace = jnp.concatenate([lax.slice_in_dim(lower_trace, 1, count, axis=4), empty], axis=4)
    prev_trace = jnp.concatenate([empty, lax.slice_in_dim(upper_trace, 0, count - 1, axis=4)], axis=4)
    tendency = add_faces(tendency, upper_trace, lower_trace, interface_flux(upper_trace, next_trace, 2), interface_flux(prev_trace, lower_trace, 2), 2)
    return tendency

def reference(state, wake_planes, bar_offsets):
    matrix = derivative_matrix()
    blocks = EPT // EP
    heads = wake_planes.shape[:3]

    def inlet_for(section_idx):
        grouped = wake_planes.reshape(heads + (blocks, EP, EST))
        grouped = jnp.roll(grouped, section_idx + 1, axis=3)
        grouped = jnp.roll(grouped, bar_offsets[section_idx], axis=4)
        return grouped.reshape(heads + (EPT, EST))
    first = state + TIME_STEP * tendency_of(state, matrix, inlet_for(0))
    second = 0.75 * state + 0.25 * (first + TIME_STEP * tendency_of(first, matrix, inlet_for(1)))
    return 1.0 / 3.0 * state + 2.0 / 3.0 * (second + TIME_STEP * tendency_of(second, matrix, inlet_for(2)))
```

```python
import functools

import jax
import jax.numpy as jnp
import numpy as np
from jax import lax
from jax.experimental import pallas as pl
from jax.experimental.pallas import tpu as pltpu
from jax.sharding import PartitionSpec as P

MEAN = (0.5, 0.3, 0.0)
SPEED = (1.5, 1.3, 1.0)
SIZE = (1.0, 0.8, 1.2)
END = 0.1
DT = 0.01
STAGES = ((0.0, 1.0), (0.75, 0.25), (1.0 / 3.0, 2.0 / 3.0))
MESH = pl.DeviceIdType.MESH
F32 = jnp.float32
VS, AS, PS, SS = 250, 50, 10, 2
ROWS = 1256


def derivative_matrix():
    x = np.array([-1.0, -np.sqrt(3.0 / 7.0), 0.0, np.sqrt(3.0 / 7.0), 1.0])
    c = np.array([np.prod([x[j] - x[k] for k in range(5) if k != j]) for j in range(5)])
    d = np.zeros((5, 5))
    for i in range(5):
        for j in range(5):
            if i != j:
                d[i, j] = c[i] / (c[j] * (x[i] - x[j]))
        d[i, i] = sum(1.0 / (x[i] - x[k]) for k in range(5) if k != i)
    d[4, 4] -= 0.5 / END
    d[0, 0] += 0.5 / END
    return d


MATRIX = derivative_matrix()


def derive(f, scale):
    d = MATRIX * scale
    s0, m0, s1, m1 = f[0] + f[4], f[0] - f[4], f[1] + f[3], f[1] - f[3]
    out = [None] * 5
    for i in range(2):
        odd = (
            float((d[i, 0] + d[i, 4]) / 2) * s0
            + float((d[i, 1] + d[i, 3]) / 2) * s1
            + float(d[i, 2]) * f[2]
        )
        even = float((d[i, 0] - d[i, 4]) / 2) * m0 + float((d[i, 1] - d[i, 3]) / 2) * m1
        out[i] = even + odd
        out[4 - i] = even - odd
    out[2] = float(d[2, 0]) * m0 + float(d[2, 1]) * m1
    return out


def others(direction):
    return [v for v in (1, 2, 3) if v != 1 + direction]


def minus_part(v, direction, h):
    o1, o2 = others(direction)
    n = v[1 + direction]
    return [h * (v[0] - n), h * (n - v[4]), h * v[o1], h * v[o2]]


def plus_part(v, direction, h):
    o1, o2 = others(direction)
    n, g = v[1 + direction], h * (SPEED[direction] + MEAN[direction])
    if direction == 2:
        both = h * (v[0] + n)
        return [both, h * (n + v[4]), h * v[o1], h * v[o2]]
    return [g * v[0] + h * n, g * n + h * v[4], g * v[o1], g * v[o2], g * v[4] + h * n]


def spread(parts, direction, upper):
    o1, o2 = others(direction)
    out = [None] * 5
    out[0], out[1 + direction], out[o1], out[o2] = parts[:4]
    if upper:
        out[4] = -parts[1]
    elif direction == 2:
        out[4] = parts[1]
    else:
        out[4] = parts[4]
    return out


class Stage:
    def __init__(self, index):
        self.alpha, self.beta = STAGES[index]
        self.bdt = self.beta * DT
        self.k = [-self.bdt * 2.0 / h for h in SIZE]
        self.h = [0.5 * self.bdt * 2.0 / (h * END) for h in SIZE]


def axial_pass(st, v_ref, s_ref, w_ref):
    lane = lax.broadcasted_iota(jnp.int32, (8, 128), 1)
    first, last = lane == 0, lane == 127
    h, k, u = st.h[0], st.k[0], MEAN[0]

    @pl.loop(0, 7)
    def _(i):
        r0 = jnp.minimum(8 * i, 42)
        rows = lambda v, a: pl.ds(v * VS + a * AS + r0, 8)
        f = [[v_ref[rows(v, a), :] for a in range(5)] for v in range(5)]
        g = [
            derive([u * f[0][a] + f[1][a] for a in range(5)], k),
            derive([u * f[1][a] + f[4][a] for a in range(5)], k),
            derive(f[2], k * u),
            derive(f[3], k * u),
            derive([u * f[4][a] + f[1][a] for a in range(5)], k),
        ]
        lo, up = [f[v][0] for v in range(5)], [f[v][4] for v in range(5)]
        mine = minus_part(up, 0, h)
        nxt = [
            jnp.where(last, own, pltpu.roll(q, 127, 1))
            for q, own in zip(minus_part(lo, 0, h), mine)
        ]
        prv = [jnp.where(first, 0.0, pltpu.roll(q, 1, 1)) for q in plus_part(up, 0, h)]
        nxt, prv = spread(nxt, 0, True), spread(prv, 0, False)
        for v in range(5):
            for a in range(5):
                diag = st.beta - (h * SPEED[0] if a in (0, 4) else 0.0)
                acc = diag * f[v][a] + g[v][a]
                if st.alpha:
                    acc = acc + st.alpha * s_ref[rows(v, a), :]
                if a == 0:
                    acc = acc + prv[v]
                if a == 4:
                    acc = acc + nxt[v]
                w_ref[rows(v, a), :] = acc


def pitch_pass(st, v_ref, w_ref):
    h, k, u = st.h[1], st.k[1], MEAN[1]
    for r0, n in ((0, 8), (8, 2)):
        even = lax.broadcasted_iota(jnp.int32, (n, 128), 0) % 2 == 0

        @pl.loop(0, 5)
        def _(a):
            rows = lambda v, p, off=0: pl.ds(v * VS + a * AS + p * PS + r0 + off, n)
            f = [[v_ref[rows(v, p), :] for p in range(5)] for v in range(5)]
            g = [
                derive([u * f[0][p] + f[2][p] for p in range(5)], k),
                derive(f[1], k * u),
                derive([u * f[2][p] + f[4][p] for p in range(5)], k),
                derive(f[3], k * u),
                derive([u * f[4][p] + f[2][p] for p in range(5)], k),
            ]
            lo = [v_ref[rows(v, 0, 1), :] for v in range(5)]
            up = [v_ref[rows(v, 4, -1), :] for v in range(5)]
            nxt = spread([jnp.where(even, q, 0.0) for q in minus_part(lo, 1, h)], 1, True)
            prv = spread([jnp.where(even, 0.0, q) for q in plus_part(up, 1, h)], 1, False)
            for v in range(5):
                for p in range(5):
                    acc = w_ref[rows(v, p), :] + g[v][p]
                    if p == 0:
                        acc = acc + prv[v] - (h * SPEED[1]) * f[v][0]
                    if p == 4:
                        acc = acc + nxt[v] - (h * SPEED[1]) * f[v][4]
                    w_ref[rows(v, p), :] = acc


def span_rows(v, s, k):
    return pl.ds(v * VS + s * SS + k, 25, PS)


def span_pass(st, v_ref, w_ref):
    h, k = st.h[2], st.k[2]
    for c in range(2):
        un = [v_ref[span_rows(3, s, c), :] for s in range(5)]
        pr = [v_ref[span_rows(4, s, c), :] for s in range(5)]
        g, gp = derive(un, k), derive(pr, k)
        for s in range(5):
            for v in range(5):
                acc = w_ref[span_rows(v, s, c), :]
                if v in (0, 4):
                    acc = acc + g[s]
                if v == 3:
                    acc = acc + gp[s]
                if s in (0, 4):
                    own = un[s] if v == 3 else pr[s] if v == 4 else v_ref[span_rows(v, s, c), :]
                    acc = acc - (h * SPEED[2]) * own
                elif v in (1, 2):
                    continue
                w_ref[span_rows(v, s, c), :] = acc


def span_message(st, v_ref, down_ref, up_ref):
    for c in range(2):
        lo = [v_ref[span_rows(v, 0, c), :] for v in range(5)]
        up = [v_ref[span_rows(v, 4, c), :] for v in range(5)]
        for j, q in enumerate(minus_part(lo, 2, st.h[2])):
            down_ref[pl.ds((2 * j + c) * 25, 25), :] = q
        for j, q in enumerate(plus_part(up, 2, st.h[2])):
            up_ref[pl.ds((2 * j + c) * 25, 25), :] = q


def span_apply(w_ref, msg_ref, upper):
    s = 4 if upper else 0
    for c in range(2):
        parts = [msg_ref[pl.ds((2 * j + c) * 25, 25), :] for j in range(4)]
        for v, q in enumerate(spread(parts, 2, upper)):
            w_ref[span_rows(v, s, c), :] = w_ref[span_rows(v, s, c), :] + q


def pitch_rows(v, a, p, c):
    return pl.ds(v * VS + a * AS + p * PS + c, 5, SS)


def pitch_message(st, v_ref, down_ref, up_ref):
    @pl.loop(0, 5)
    def _(a):
        lo = [v_ref[pitch_rows(v, a, 0, 0), :] for v in range(5)]
        up = [v_ref[pitch_rows(v, a, 4, 1), :] for v in range(5)]
        for j, q in enumerate(minus_part(lo, 1, st.h[1])):
            down_ref[pl.ds(j * 25 + a * 5, 5), :] = q
        for j, q in enumerate(plus_part(up, 1, st.h[1])):
            up_ref[pl.ds(j * 25 + a * 5, 5), :] = q


def pitch_apply(w_ref, msg_ref, upper):
    p, c, n = (4, 1, 4) if upper else (0, 0, 5)

    @pl.loop(0, 5)
    def _(a):
        parts = [msg_ref[pl.ds(j * 25 + a * 5, 5), :] for j in range(n)]
        for v, q in enumerate(spread(parts, 1, upper)):
            w_ref[pitch_rows(v, a, p, c), :] = w_ref[pitch_rows(v, a, p, c), :] + q


def pack_wake(wake_ref, tmp_ref, out_ref):
    lane = lax.broadcasted_iota(jnp.int32, (2, 128), 1)
    total = jnp.zeros((2, 128), F32)
    for i in range(25):
        tmp_ref[i, :, 0:5] = wake_ref[i]
    for i in range(25):
        tile = jnp.where(lane < 5, tmp_ref[i], 0.0)
        total = total + (pltpu.roll(tile, 5 * i, 1) if i else tile)
    out_ref[...] = total


def wake_apply(st, w_ref, wake_ref, offset):
    row = lax.broadcasted_iota(jnp.int32, (50, 128), 0)
    lane = lax.broadcasted_iota(jnp.int32, (50, 128), 1)
    flip = (row + offset) % 2 == 0
    tile = wake_ref[...]
    chosen = jnp.where(
        flip, jnp.broadcast_to(tile[0:1], (50, 128)), jnp.broadcast_to(tile[1:2], (50, 128))
    )
    g = []
    for v in range(5):
        picked = jnp.where(lane == v * 25 + row // 2, chosen, 0.0)
        g.append(jnp.broadcast_to(jnp.sum(picked, axis=1, keepdims=True), (50, 128)))
    parts = spread(plus_part(g, 0, st.h[0]), 0, False)
    for v in range(5):
        rows = pl.ds(v * VS, 50)
        w_ref[rows, :] = w_ref[rows, :] + jnp.where(lane == 0, parts[v], 0.0)


def kernel(
    np_, ns_, offs_ref, state_hbm, wake_ref, out_hbm,
    s_ref, w1_ref, w2_ref, w3_ref, tmp_ref, own_wake, got_wake,
    p_down, p_up, s_down, s_up, r_next, r_prev, t_next, t_prev,
    send_sem, recv_sem, wake_send, wake_recv, io_sem,
):
    ip, js = lax.axis_index("pitch"), lax.axis_index("span")
    p_next, p_prev = lax.rem(ip + 1, np_), lax.rem(ip + np_ - 1, np_)
    has_next, has_prev = js < ns_ - 1, js > 0
    load = pltpu.make_async_copy(
        state_hbm.reshape(1250, 128), s_ref.at[pl.ds(0, 1250)], io_sem.at[0]
    )
    load.start()

    barrier = pltpu.get_barrier_semaphore()
    for q in (p_next, p_prev):
        pl.semaphore_signal(barrier, inc=1, device_id={"pitch": q}, device_id_type=MESH)

    @pl.when(has_next)
    def _():
        pl.semaphore_signal(barrier, inc=1, device_id={"span": js + 1}, device_id_type=MESH)

    @pl.when(has_prev)
    def _():
        pl.semaphore_signal(barrier, inc=1, device_id={"span": js - 1}, device_id_type=MESH)

    pack_wake(wake_ref, tmp_ref, own_wake)
    load.wait()
    pl.semaphore_wait(
        barrier, 2 + has_next.astype(jnp.int32) + has_prev.astype(jnp.int32)
    )

    def remote(src, dst, n, way, device):
        return pltpu.make_async_remote_copy(
            src_ref=src, dst_ref=dst, send_sem=send_sem.at[n, way], recv_sem=recv_sem.at[n, way],
            device_id=device, device_id_type=MESH,
        )

    def wake_copy(n):
        return pltpu.make_async_remote_copy(
            src_ref=own_wake if n == 0 else got_wake.at[n - 1], dst_ref=got_wake.at[n],
            send_sem=wake_send.at[n], recv_sem=wake_recv.at[n],
            device_id={"pitch": p_next}, device_id_type=MESH,
        )

    values = [s_ref, w1_ref, w2_ref, w3_ref]
    wake_copy(0).start()
    copies = []
    for n in range(3):
        st, v_ref, w_ref = Stage(n), values[n], values[n + 1]
        to_next = remote(p_up.at[n], r_prev.at[n], n, 0, {"pitch": p_next})
        to_prev = remote(p_down.at[n], r_next.at[n], n, 1, {"pitch": p_prev})
        to_above = remote(s_up.at[n], t_prev.at[n], n, 2, {"span": js + 1})
        to_below = remote(s_down.at[n], t_next.at[n], n, 3, {"span": js - 1})
        pitch_message(st, v_ref, p_down.at[n], p_up.at[n])
        to_next.start()
        to_prev.start()
        span_message(st, v_ref, s_down.at[n], s_up.at[n])
        pl.when(has_next)(to_above.start)
        pl.when(has_prev)(to_below.start)

        axial_pass(st, v_ref, s_ref, w_ref)
        pitch_pass(st, v_ref, w_ref)
        span_pass(st, v_ref, w_ref)
        wake_copy(n).wait_recv()
        if n < 2:
            wake_copy(n + 1).start()
        wake_apply(st, w_ref, got_wake.at[n], offs_ref[n])

        @pl.when(has_prev)
        def _():
            to_above.wait_recv()
            span_apply(w_ref, t_prev.at[n], False)

        @pl.when(has_next)
        def _():
            to_below.wait_recv()
            span_apply(w_ref, t_next.at[n], True)

        to_next.wait_recv()
        pitch_apply(w_ref, r_prev.at[n], False)
        to_prev.wait_recv()
        pitch_apply(w_ref, r_next.at[n], True)
        copies.append((to_next, to_prev, to_above, to_below))

    store = pltpu.make_async_copy(
        w3_ref.at[pl.ds(0, 1250)], out_hbm.reshape(1250, 128), io_sem.at[1]
    )
    store.start()
    for n, (to_next, to_prev, to_above, to_below) in enumerate(copies):
        wake_copy(n).wait_send()
        to_next.wait_send()
        to_prev.wait_send()
        pl.when(has_next)(to_above.wait_send)
        pl.when(has_prev)(to_below.wait_send)
    store.wait()


def solution(mesh):
    np_, ns_ = mesh.shape["pitch"], mesh.shape["span"]

    def step(state, wake, offsets):
        flat = state.reshape(625, 2, 128)
        rows = jnp.transpose(wake, (0, 1, 3, 4, 2)).reshape(25, 2, 5)
        out = pl.pallas_call(
            functools.partial(kernel, np_, ns_),
            out_shape=jax.ShapeDtypeStruct((625, 2, 128), F32),
            in_specs=[
                pl.BlockSpec(memory_space=pltpu.SMEM),
                pl.BlockSpec(memory_space=pl.ANY),
                pl.BlockSpec(memory_space=pltpu.VMEM),
            ],
            out_specs=pl.BlockSpec(memory_space=pl.ANY),
            scratch_shapes=[pltpu.VMEM((ROWS, 128), F32)] * 4
            + [
                pltpu.VMEM((25, 2, 128), F32),
                pltpu.VMEM((2, 128), F32),
                pltpu.VMEM((3, 2, 128), F32),
                pltpu.VMEM((3, 100, 128), F32),
                pltpu.VMEM((3, 125, 128), F32),
                pltpu.VMEM((3, 200, 128), F32),
                pltpu.VMEM((3, 200, 128), F32),
                pltpu.VMEM((3, 100, 128), F32),
                pltpu.VMEM((3, 125, 128), F32),
                pltpu.VMEM((3, 200, 128), F32),
                pltpu.VMEM((3, 200, 128), F32),
                pltpu.SemaphoreType.DMA((3, 4)),
                pltpu.SemaphoreType.DMA((3, 4)),
                pltpu.SemaphoreType.DMA((3,)),
                pltpu.SemaphoreType.DMA((3,)),
                pltpu.SemaphoreType.DMA((2,)),
            ],
            compiler_params=pltpu.CompilerParams(collective_id=0, has_side_effects=True),
        )(offsets, flat, rows)
        return out.reshape(state.shape)

    spec = P(None, None, None, None, "pitch", "span", None)
    return jax.shard_map(
        step,
        mesh=mesh,
        in_specs=(spec, P(None, None, None, "pitch", "span"), P()),
        out_specs=spec,
        check_vma=False,
    )
```

```python
import functools

import jax
import jax.numpy as jnp
import numpy as np
from jax import lax
from jax.experimental import pallas as pl
from jax.experimental.pallas import tpu as pltpu
from jax.sharding import PartitionSpec as P

MEAN = (0.5, 0.3, 0.0)
SPEED = (1.5, 1.3, 1.0)
SIZE = (1.0, 0.8, 1.2)
END = 0.1
DT = 0.01
STAGES = ((0.0, 1.0), (0.75, 0.25), (1.0 / 3.0, 2.0 / 3.0))
MESH = pl.DeviceIdType.MESH
F32 = jnp.float32
VS, AS, PS, SS = 250, 50, 10, 2
ROWS = 1408
FAR = 16


def derivative_matrix():
    x = np.array([-1.0, -np.sqrt(3.0 / 7.0), 0.0, np.sqrt(3.0 / 7.0), 1.0])
    c = np.array([np.prod([x[j] - x[k] for k in range(5) if k != j]) for j in range(5)])
    d = np.zeros((5, 5))
    for i in range(5):
        for j in range(5):
            if i != j:
                d[i, j] = c[i] / (c[j] * (x[i] - x[j]))
        d[i, i] = sum(1.0 / (x[i] - x[k]) for k in range(5) if k != i)
    d[4, 4] -= 0.5 / END
    d[0, 0] += 0.5 / END
    return d


MATRIX = derivative_matrix()


def derive(f, scale):
    d = MATRIX * scale
    s0, m0, s1, m1 = f[0] + f[4], f[0] - f[4], f[1] + f[3], f[1] - f[3]
    out = [None] * 5
    for i in range(2):
        odd = (
            float((d[i, 0] + d[i, 4]) / 2) * s0
            + float((d[i, 1] + d[i, 3]) / 2) * s1
            + float(d[i, 2]) * f[2]
        )
        even = float((d[i, 0] - d[i, 4]) / 2) * m0 + float((d[i, 1] - d[i, 3]) / 2) * m1
        out[i] = even + odd
        out[4 - i] = even - odd
    out[2] = float(d[2, 0]) * m0 + float(d[2, 1]) * m1
    return out


def others(direction):
    return [v for v in (1, 2, 3) if v != 1 + direction]


def minus_part(v, direction, h):
    o1, o2 = others(direction)
    n = v[1 + direction]
    return [h * (v[0] - n), h * (n - v[4]), h * v[o1], h * v[o2]]


def plus_part(v, direction, h):
    o1, o2 = others(direction)
    n, g = v[1 + direction], h * (SPEED[direction] + MEAN[direction])
    if direction == 2:
        both = h * (v[0] + n)
        return [both, h * (n + v[4]), h * v[o1], h * v[o2]]
    return [g * v[0] + h * n, g * n + h * v[4], g * v[o1], g * v[o2], g * v[4] + h * n]


def spread(parts, direction, upper):
    o1, o2 = others(direction)
    out = [None] * 5
    out[0], out[1 + direction], out[o1], out[o2] = parts[:4]
    if upper:
        out[4] = -parts[1]
    elif direction == 2:
        out[4] = parts[1]
    else:
        out[4] = parts[4]
    return out


class Stage:
    def __init__(self, index, carry=True):
        self.alpha, self.beta = STAGES[index]
        if not carry:
            self.alpha = 0.0
        self.bdt = self.beta * DT
        self.k = [-self.bdt * 2.0 / h for h in SIZE]
        self.h = [0.5 * self.bdt * 2.0 / (h * END) for h in SIZE]


def axial_pass(st, v_ref, s_ref, w_ref):
    lane = lax.broadcasted_iota(jnp.int32, (8, 128), 1)
    first, last = lane == 0, lane == 127
    h, k, u = st.h[0], st.k[0], MEAN[0]

    @pl.loop(0, 7)
    def _(i):
        r0 = jnp.minimum(8 * i, 42)
        rows = lambda v, a: pl.ds(v * VS + a * AS + r0, 8)
        f = [[v_ref[rows(v, a), :] for a in range(5)] for v in range(5)]
        g = [
            derive([u * f[0][a] + f[1][a] for a in range(5)], k),
            derive([u * f[1][a] + f[4][a] for a in range(5)], k),
            derive(f[2], k * u),
            derive(f[3], k * u),
            derive([u * f[4][a] + f[1][a] for a in range(5)], k),
        ]
        lo, up = [f[v][0] for v in range(5)], [f[v][4] for v in range(5)]
        mine = minus_part(up, 0, h)
        nxt = [
            jnp.where(last, own, pltpu.roll(q, 127, 1))
            for q, own in zip(minus_part(lo, 0, h), mine)
        ]
        prv = [jnp.where(first, 0.0, pltpu.roll(q, 1, 1)) for q in plus_part(up, 0, h)]
        nxt, prv = spread(nxt, 0, True), spread(prv, 0, False)
        for v in range(5):
            for a in range(5):
                diag = st.beta - (h * SPEED[0] if a in (0, 4) else 0.0)
                acc = diag * f[v][a] + g[v][a]
                if st.alpha:
                    acc = acc + st.alpha * s_ref[rows(v, a), :]
                if a == 0:
                    acc = acc + prv[v]
                if a == 4:
                    acc = acc + nxt[v]
                w_ref[rows(v, a), :] = acc


def pitch_pass(st, v_ref, w_ref):
    h, k, u = st.h[1], st.k[1], MEAN[1]
    for r0, n in ((0, 8), (8, 2)):
        even = lax.broadcasted_iota(jnp.int32, (n, 128), 0) % 2 == 0

        @pl.loop(0, 5)
        def _(a):
            rows = lambda v, p, off=0: pl.ds(v * VS + a * AS + p * PS + r0 + off, n)
            f = [[v_ref[rows(v, p), :] for p in range(5)] for v in range(5)]
            g = [
                derive([u * f[0][p] + f[2][p] for p in range(5)], k),
                derive(f[1], k * u),
                derive([u * f[2][p] + f[4][p] for p in range(5)], k),
                derive(f[3], k * u),
                derive([u * f[4][p] + f[2][p] for p in range(5)], k),
            ]
            lo = [v_ref[rows(v, 0, 1), :] for v in range(5)]
            up = [v_ref[rows(v, 4, -1), :] for v in range(5)]
            nxt = spread([jnp.where(even, q, 0.0) for q in minus_part(lo, 1, h)], 1, True)
            prv = spread([jnp.where(even, 0.0, q) for q in plus_part(up, 1, h)], 1, False)
            for v in range(5):
                for p in range(5):
                    acc = w_ref[rows(v, p), :] + g[v][p]
                    if p == 0:
                        acc = acc + prv[v] - (h * SPEED[1]) * f[v][0]
                    if p == 4:
                        acc = acc + nxt[v] - (h * SPEED[1]) * f[v][4]
                    w_ref[rows(v, p), :] = acc


def span_rows(v, s, k):
    return pl.ds(v * VS + s * SS + k, 25, PS)


def span_pass(st, v_ref, w_ref):
    h, k = st.h[2], st.k[2]
    for c in range(2):
        un = [v_ref[span_rows(3, s, c), :] for s in range(5)]
        pr = [v_ref[span_rows(4, s, c), :] for s in range(5)]
        g, gp = derive(un, k), derive(pr, k)
        for s in range(5):
            for v in range(5):
                acc = w_ref[span_rows(v, s, c), :]
                if v in (0, 4):
                    acc = acc + g[s]
                if v == 3:
                    acc = acc + gp[s]
                if s in (0, 4):
                    own = un[s] if v == 3 else pr[s] if v == 4 else v_ref[span_rows(v, s, c), :]
                    acc = acc - (h * SPEED[2]) * own
                elif v in (1, 2):
                    continue
                w_ref[span_rows(v, s, c), :] = acc


def span_message(st, v_ref, down_ref, up_ref):
    for c in range(2):
        lo = [v_ref[span_rows(v, 0, c), :] for v in range(5)]
        up = [v_ref[span_rows(v, 4, c), :] for v in range(5)]
        for j, q in enumerate(minus_part(lo, 2, st.h[2])):
            down_ref[pl.ds((2 * j + c) * 25, 25), :] = q
        for j, q in enumerate(plus_part(up, 2, st.h[2])):
            up_ref[pl.ds((2 * j + c) * 25, 25), :] = q


def span_apply(w_ref, msg_ref, upper):
    s = 4 if upper else 0
    for c in range(2):
        parts = [msg_ref[pl.ds((2 * j + c) * 25, 25), :] for j in range(4)]
        for v, q in enumerate(spread(parts, 2, upper)):
            w_ref[span_rows(v, s, c), :] = w_ref[span_rows(v, s, c), :] + q


def pitch_rows(v, a, p, c):
    return pl.ds(v * VS + a * AS + p * PS + c, 5, SS)


def pitch_message(st, v_ref, down_ref, up_ref):
    @pl.loop(0, 5)
    def _(a):
        lo = [v_ref[pitch_rows(v, a, 0, 0), :] for v in range(5)]
        up = [v_ref[pitch_rows(v, a, 4, 1), :] for v in range(5)]
        for j, q in enumerate(minus_part(lo, 1, st.h[1])):
            down_ref[pl.ds(j * 25 + a * 5, 5), :] = q
        for j, q in enumerate(plus_part(up, 1, st.h[1])):
            up_ref[pl.ds(j * 25 + a * 5, 5), :] = q


def pitch_apply(w_ref, msg_ref, upper):
    p, c, n = (4, 1, 4) if upper else (0, 0, 5)

    @pl.loop(0, 5)
    def _(a):
        parts = [msg_ref[pl.ds(j * 25 + a * 5, 5), :] for j in range(n)]
        for v, q in enumerate(spread(parts, 1, upper)):
            w_ref[pitch_rows(v, a, p, c), :] = w_ref[pitch_rows(v, a, p, c), :] + q


def pack_wake(wake_ref, tmp_ref, out_ref):
    lane = lax.broadcasted_iota(jnp.int32, (2, 128), 1)
    total = jnp.zeros((2, 128), F32)
    for i in range(25):
        tmp_ref[i, :, 0:5] = wake_ref[i]
    for i in range(25):
        tile = jnp.where(lane < 5, tmp_ref[i], 0.0)
        total = total + (pltpu.roll(tile, 5 * i, 1) if i else tile)
    out_ref[...] = total


def wake_apply(st, w_ref, wake_ref, offset):
    row = lax.broadcasted_iota(jnp.int32, (50, 128), 0)
    lane = lax.broadcasted_iota(jnp.int32, (50, 128), 1)
    flip = (row + offset) % 2 == 0
    tile = wake_ref[...]
    chosen = jnp.where(
        flip, jnp.broadcast_to(tile[0:1], (50, 128)), jnp.broadcast_to(tile[1:2], (50, 128))
    )
    g = []
    for v in range(5):
        picked = jnp.where(lane == v * 25 + row // 2, chosen, 0.0)
        g.append(jnp.broadcast_to(jnp.sum(picked, axis=1, keepdims=True), (50, 128)))
    parts = spread(plus_part(g, 0, st.h[0]), 0, False)
    for v in range(5):
        rows = pl.ds(v * VS, 50)
        w_ref[rows, :] = w_ref[rows, :] + jnp.where(lane == 0, parts[v], 0.0)


EDGES = ((0, 0), (4, 1))


def edge_rows(v, s, i):
    p, c = EDGES[i]
    return pl.ds(v * VS + p * PS + s * SS + c, 5, AS)


def edge_message(st, v_ref, down_ref, up_ref):
    for i in range(2):
        lo = [v_ref[edge_rows(v, 0, i), :] for v in range(5)]
        up = [v_ref[edge_rows(v, 4, i), :] for v in range(5)]
        for j, q in enumerate(minus_part(lo, 2, st.h[2])):
            down_ref[pl.ds((2 * j + i) * 5, 5), :] = q
        for j, q in enumerate(plus_part(up, 2, st.h[2])):
            up_ref[pl.ds((2 * j + i) * 5, 5), :] = q


def edge_apply(w_ref, msg_ref, upper):
    s = 4 if upper else 0
    for i in range(2):
        parts = [msg_ref[pl.ds((2 * j + i) * 5, 5), :] for j in range(4)]
        for v, q in enumerate(spread(parts, 2, upper)):
            w_ref[edge_rows(v, s, i), :] = w_ref[edge_rows(v, s, i), :] + q


def volume(st, v_ref, s_ref, w_ref):
    axial_pass(st, v_ref, s_ref, w_ref)
    pitch_pass(st, v_ref, w_ref)
    span_pass(st, v_ref, w_ref)


def add_rows(a_ref, b_ref, w_ref):
    @pl.loop(0, 157)
    def _(i):
        rows = pl.ds(pl.multiple_of(8 * i, 8), 8)
        w_ref[rows, :] = a_ref[rows, :] + b_ref[rows, :]


def kernel(
    np_, ns_, offs_ref, state_hbm, wake_ref, t3_ref,
    s_ref, w1_ref, w2_ref, x1_ref, x2_ref, c1_ref, c2_ref, t_ref,
    tmp_ref, own_wake, got_wake,
    p_down, p_up, s_down, s_up, r_next, r_prev, t_next, t_prev,
    l_down, l_up, e_down, e_up, e_next, e_prev,
    send_sem, recv_sem, edge_send, edge_recv, wake_send, wake_recv, io_sem,
):
    ip, js = lax.axis_index("pitch"), lax.axis_index("span")
    p_next, p_prev = lax.rem(ip + 1, np_), lax.rem(ip + np_ - 1, np_)
    has_next, has_prev = js < ns_ - 1, js > 0
    load = pltpu.make_async_copy(
        state_hbm.reshape(1250, 128), s_ref.at[pl.ds(0, 1250)], io_sem.at[0]
    )
    load.start()

    barrier = pltpu.get_barrier_semaphore()
    for q in (p_next, p_prev):
        pl.semaphore_signal(barrier, inc=1, device_id={"pitch": q}, device_id_type=MESH)

    @pl.when(has_next)
    def _():
        pl.semaphore_signal(barrier, inc=1, device_id={"span": js + 1}, device_id_type=MESH)

    @pl.when(has_prev)
    def _():
        pl.semaphore_signal(barrier, inc=1, device_id={"span": js - 1}, device_id_type=MESH)

    pack_wake(wake_ref, tmp_ref, own_wake)
    pl.semaphore_wait(
        barrier, 2 + has_next.astype(jnp.int32) + has_prev.astype(jnp.int32)
    )

    def remote(src, dst, sends, recvs, device):
        return pltpu.make_async_remote_copy(
            src_ref=src, dst_ref=dst, send_sem=sends, recv_sem=recvs,
            device_id=device, device_id_type=MESH,
        )

    def wake_copy(n):
        return remote(
            own_wake if n == 0 else got_wake.at[n - 1], got_wake.at[n],
            wake_send.at[n], wake_recv.at[n], {"pitch": p_next},
        )

    def pitch_copies(n):
        return (
            remote(p_up.at[n, pl.ds(0, 125)], r_prev.at[n, pl.ds(0, 125)], send_sem.at[n, 0], recv_sem.at[n, 0], {"pitch": p_next}),
            remote(p_down.at[n, pl.ds(0, 100)], r_next.at[n, pl.ds(0, 100)], send_sem.at[n, 1], recv_sem.at[n, 1], {"pitch": p_prev}),
        )

    def span_copies(n):
        return (
            remote(s_up.at[n, pl.ds(0, 200)], t_prev.at[n, pl.ds(0, 200)], send_sem.at[n, 2], recv_sem.at[n, 2], {"span": js + 1}),
            remote(s_down.at[n, pl.ds(0, 200)], t_next.at[n, pl.ds(0, 200)], send_sem.at[n, 3], recv_sem.at[n, 3], {"span": js - 1}),
        )

    def edge_copies(n):
        return (
            remote(e_up.at[n, pl.ds(0, 40)], e_prev.at[n, pl.ds(0, 40)], edge_send.at[n, 0], edge_recv.at[n, 0], {"span": js + 1}),
            remote(e_down.at[n, pl.ds(0, 40)], e_next.at[n, pl.ds(0, 40)], edge_send.at[n, 1], edge_recv.at[n, 1], {"span": js - 1}),
        )

    def span_start(above, below):
        pl.when(has_next)(above.start)
        pl.when(has_prev)(below.start)

    def span_receive(above, below, apply, w_ref, prev_ref, next_ref):
        @pl.when(has_prev)
        def _():
            above.wait_recv()
            apply(w_ref, prev_ref, False)

        @pl.when(has_next)
        def _():
            below.wait_recv()
            apply(w_ref, next_ref, True)

    pitch, span = [pitch_copies(n) for n in range(3)], [span_copies(n) for n in range(3)]
    edges = [edge_copies(n) for n in range(2)]

    wake_copy(0).start()
    stages = [Stage(n) for n in range(3)]
    linear = Stage(1, carry=False)
    load.wait()
    pitch_message(stages[0], s_ref, p_down.at[0], p_up.at[0])
    for copy in pitch[0]:
        copy.start()
    span_message(stages[0], s_ref, s_down.at[0], s_up.at[0])
    span_start(*span[0])
    x1_ref[...] = jnp.zeros((ROWS, 128), F32)
    c1_ref[...] = jnp.zeros((ROWS, 128), F32)
    pitch_apply(x1_ref, p_down.at[0], True)
    pitch_apply(x1_ref, p_up.at[0], False)
    edge_message(linear, x1_ref, e_down.at[0], e_up.at[0])
    span_start(*edges[0])

    volume(stages[0], s_ref, s_ref, w1_ref)
    volume(linear, x1_ref, s_ref, x2_ref)
    wake_copy(0).wait_recv()
    wake_copy(1).start()
    wake_apply(stages[0], w1_ref, got_wake.at[0], offs_ref[0])
    span_receive(*span[0], span_apply, w1_ref, t_prev.at[0], t_next.at[0])
    span_message(stages[1], w1_ref, s_down.at[1], s_up.at[1])
    span_start(*span[1])
    pitch_message(stages[1], w1_ref, p_down.at[1], p_up.at[1])
    for copy in pitch[1]:
        copy.start()
    volume(stages[1], w1_ref, s_ref, w2_ref)
    wake_copy(1).wait_recv()
    wake_copy(2).start()
    wake_apply(stages[1], w2_ref, got_wake.at[1], offs_ref[1])

    def finish_second():
        span_receive(*span[1], span_apply, w2_ref, t_prev.at[1], t_next.at[1])
        pitch_message(stages[2], w2_ref, p_down.at[2], p_up.at[2])
        for copy in pitch[2]:
            copy.start()

    far = lax.rem(ip, FAR) == FAR - 1
    pl.when(far)(finish_second)

    pitch[0][0].wait_recv()
    pitch_apply(c1_ref, r_prev.at[0], False)
    pitch[0][1].wait_recv()
    pitch_apply(c1_ref, r_next.at[0], True)
    edge_message(linear, c1_ref, e_down.at[1], e_up.at[1])
    span_start(*edges[1])
    add_rows(w1_ref, c1_ref, t_ref)
    span_receive(*edges[0], edge_apply, x2_ref, e_prev.at[0], e_next.at[0])
    pitch_message(stages[1], t_ref, l_down, l_up)
    pitch_apply(x2_ref, l_down, True)
    pitch_apply(x2_ref, l_up, False)
    volume(linear, c1_ref, s_ref, c2_ref)
    pitch_message(stages[1], x1_ref, l_down, l_up)
    pitch_apply(c2_ref, l_down, True)
    pitch_apply(c2_ref, l_up, False)
    pl.when(jnp.logical_not(far))(finish_second)
    span_receive(*edges[1], edge_apply, c2_ref, e_prev.at[1], e_next.at[1])
    pitch[1][0].wait_recv()
    pitch_apply(c2_ref, r_prev.at[1], False)
    pitch[1][1].wait_recv()
    pitch_apply(c2_ref, r_next.at[1], True)
    add_rows(w2_ref, c2_ref, t_ref)

    span_message(stages[2], t_ref, s_down.at[2], s_up.at[2])
    span_start(*span[2])
    volume(stages[2], t_ref, s_ref, t3_ref)
    wake_copy(2).wait_recv()
    wake_apply(stages[2], t3_ref, got_wake.at[2], offs_ref[2])
    pitch_message(stages[2], x2_ref, l_down, l_up)
    pitch_apply(t3_ref, l_down, True)
    pitch_apply(t3_ref, l_up, False)
    span_receive(*span[2], span_apply, t3_ref, t_prev.at[2], t_next.at[2])
    pitch[2][0].wait_recv()
    pitch_apply(t3_ref, r_prev.at[2], False)
    pitch[2][1].wait_recv()
    pitch_apply(t3_ref, r_next.at[2], True)

    for n in range(3):
        wake_copy(n).wait_send()
        for copy in pitch[n]:
            copy.wait_send()
    for above, below in span + edges:
        pl.when(has_next)(above.wait_send)
        pl.when(has_prev)(below.wait_send)


def store_kernel(rows_ref, out_hbm, sem):
    copy = pltpu.make_async_copy(rows_ref.at[pl.ds(0, 1250)], out_hbm.reshape(1250, 128), sem)
    copy.start()
    copy.wait()


def solution(mesh):
    np_, ns_ = mesh.shape["pitch"], mesh.shape["span"]

    def step(state, wake, offsets):
        flat = state.reshape(625, 2, 128)
        rows = jnp.transpose(wake, (0, 1, 3, 4, 2)).reshape(25, 2, 5)
        out = pl.pallas_call(
            functools.partial(kernel, np_, ns_),
            out_shape=jax.ShapeDtypeStruct((ROWS, 128), F32),
            in_specs=[
                pl.BlockSpec(memory_space=pltpu.SMEM),
                pl.BlockSpec(memory_space=pl.ANY),
                pl.BlockSpec(memory_space=pltpu.VMEM),
            ],
            out_specs=pl.BlockSpec(memory_space=pltpu.VMEM),
            scratch_shapes=[pltpu.VMEM((ROWS, 128), F32)] * 8
            + [
                pltpu.VMEM((25, 2, 128), F32),
                pltpu.VMEM((2, 128), F32),
                pltpu.VMEM((3, 2, 128), F32),
                pltpu.VMEM((3, 112, 128), F32),
                pltpu.VMEM((3, 136, 128), F32),
                pltpu.VMEM((3, 208, 128), F32),
                pltpu.VMEM((3, 208, 128), F32),
                pltpu.VMEM((3, 112, 128), F32),
                pltpu.VMEM((3, 136, 128), F32),
                pltpu.VMEM((3, 208, 128), F32),
                pltpu.VMEM((3, 208, 128), F32),
                pltpu.VMEM((112, 128), F32),
                pltpu.VMEM((136, 128), F32),
                pltpu.VMEM((2, 48, 128), F32),
                pltpu.VMEM((2, 48, 128), F32),
                pltpu.VMEM((2, 48, 128), F32),
                pltpu.VMEM((2, 48, 128), F32),
                pltpu.SemaphoreType.DMA((3, 4)),
                pltpu.SemaphoreType.DMA((3, 4)),
                pltpu.SemaphoreType.DMA((2, 2)),
                pltpu.SemaphoreType.DMA((2, 2)),
                pltpu.SemaphoreType.DMA((3,)),
                pltpu.SemaphoreType.DMA((3,)),
                pltpu.SemaphoreType.DMA((2,)),
            ],
            compiler_params=pltpu.CompilerParams(collective_id=0, has_side_effects=True),
        )(offsets, flat, rows)
        out = pl.pallas_call(
            store_kernel,
            out_shape=jax.ShapeDtypeStruct((625, 2, 128), F32),
            in_specs=[pl.BlockSpec(memory_space=pltpu.VMEM)],
            out_specs=pl.BlockSpec(memory_space=pl.ANY),
            scratch_shapes=[pltpu.SemaphoreType.DMA],
        )(out)
        return out.reshape(state.shape)

    spec = P(None, None, None, None, "pitch", "span", None)
    return jax.shard_map(
        step,
        mesh=mesh,
        in_specs=(spec, P(None, None, None, "pitch", "span"), P()),
        out_specs=spec,
        check_vma=False,
    )
```
